32 devices in a mesh: scene: 4 (over x, core), slab: 8 (over z, y).
Axes of the slice: x: 2, y: 2, z: 4, core: 2. Of those that a mesh axis runs over, the one named last changes fastest.
Arguments:
- camera_features: bfloat16 [2048, 128, 128], P(('scene', 'slab')), parts along dimension 0, may hold values from -6 to 6
- cell_index: int32 [2048, 128], P('scene'), parts along dimension 0, may hold values from 0 to 127
- owner_device: int32 [2048, 1], P('scene'), parts along dimension 0, may hold values from 0 to 7; in each aligned block of 64 rows (0 to 63, 64 to 127, ...) at most 8 rows name the same one
- owner_tile: int32 [2048], P('scene'), parts along dimension 0, may hold values from 0 to 31
- base_map: bfloat16 [512, 256, 128], P(('scene', 'slab')), parts along dimension 0, may hold values from -6 to 6
- targets: bfloat16 [512, 256, 128], P(('scene', 'slab')), parts along dimension 0, may hold values from 0 to 1
- fine_conv: bfloat16 [1152, 128], replicated, may hold values from -0.1875 to 0.1875
- fine_down: bfloat16 [512, 256], replicated, may hold values from -0.25 to 0.25
- middle_conv: bfloat16 [2304, 256], replicated, may hold values from -0.125 to 0.125
- middle_down: bfloat16 [1024, 512], replicated, may hold values from -0.1875 to 0.1875
- coarse_conv: bfloat16 [4608, 512], replicated, may hold values from -0.09375 to 0.09375
- coarse_up: bfloat16 [512, 1024], replicated, may hold values from -0.25 to 0.25
- middle_merge: bfloat16 [2304, 256], replicated, may hold values from -0.125 to 0.125
- middle_up: bfloat16 [256, 512], replicated, may hold values from -0.375 to 0.375
- fine_merge: bfloat16 [1152, 128], replicated, may hold values from -0.1875 to 0.1875
- head_weight: bfloat16 [128, 128], replicated, may hold values from -0.5 to 0.5
Outputs:
- camera_grad: bfloat16 [2048, 128, 128], P(('scene', 'slab')), parts along dimension 0
- row_loss: float32 [512], P(('scene', 'slab')), parts along dimension 0
- fine_conv_grad: float32 [4608, 128], P(('scene', 'slab')), parts along dimension 0
- fine_down_grad: float32 [2048, 256], P(('scene', 'slab')), parts along dimension 0
- middle_conv_grad: float32 [9216, 256], P(('scene', 'slab')), parts along dimension 0
- middle_down_grad: float32 [4096, 512], P(('scene', 'slab')), parts along dimension 0
- coarse_conv_grad: float32 [18432, 512], P(('scene', 'slab')), parts along dimension 0
- coarse_up_grad: float32 [2048, 1024], P(('scene', 'slab')), parts along dimension 0
- middle_merge_grad: float32 [9216, 256], P(('scene', 'slab')), parts along dimension 0
- middle_up_grad: float32 [1024, 512], P(('scene', 'slab')), parts along dimension 0
- fine_merge_grad: float32 [4608, 128], P(('scene', 'slab')), parts along dimension 0
- head_grad: float32 [512, 128], P(('scene', 'slab')), parts along dimension 0
The draws below stay inside these ranges and needn't reach their ends.
There are 4 independent parts, one for each index of `scene`. The reference program is written for one: setup_inputs(seed, part) draws one part's arguments, and reference() takes and returns one part's arrays. A program takes and returns all parts, laid end to end along the dimension named above; an argument that names none is the same for every part. Nothing has to cross between parts.
Inputs may be any that keep to these rules, and one draw needn't show every extreme that they name: `owner_device`: of the 64 blocks in each aligned run of 64 rows (the blocks of one index of slab), at most 8 name the same index, a bound that some block reaches of them.
All inputs are finite; a program needn't handle non-finite values.
Results may differ from the reference program's by a relative error of at most 0.017.
Values may be sent and summed in bfloat16 or wider, within the bound.
No kernel may reach another device: no remote copies, remote signals or barrier semaphores. Data moves between devices by JAX's collectives and lax.ppermute only.
A program may use at most 192 MiB of HBM per device.

```python
import math
import jax
import jax.numpy as jnp
import numpy as np
from jax import lax

W = 256
BLK_DEV = 64
C0 = 128
C1 = 256
C2 = 512
K = 128
PTS = 128
TILE = 128
CAP = 8
TILES_DEV = 32
ROWS = 128
BLOCKS = 512
N_SLAB = 8


def plant(array, key, smallest, high):
    longest = array.shape.index(max(array.shape))
    spots = []
    for shift in (0, 1):
        where = [jax.random.randint(jax.random.fold_in(key, axis), (), 0, length) for axis, length in enumerate(array.shape)]
        where[longest] = (where[longest] + shift) % array.shape[longest]
        spots.append(tuple(where))
    return array.at[spots[0]].set(smallest).at[spots[1]].set(high)


def shard_levels(key, dims, cuts, smallest, top_value):
    gain, own = 1.0, jax.random.fold_in(key, 6)
    for axis_at, parts in cuts:
        draws = jnp.exp(jax.random.uniform(jax.random.fold_in(own, axis_at), (parts,), jnp.float32, smallest / len(cuts), top_value / len(cuts)))
        gain = gain * jnp.repeat(draws, dims[axis_at] // parts).reshape([-1 if axis == axis_at else 1 for axis in range(len(dims))])
    return gain


def routed_block(stream_key, own, number, rows, count, top, most, skew):
    sequence = jax.random.permutation(stream_key, count)
    heavy_load, ordinary = load_shares(count, rows * top, most, skew, True), load_shares(count, rows * top, most, skew, False)
    places = jnp.arange(count)

    def named(sizes, rotation):
        used = int((sizes > 0).sum())
        fixed = max(1, used // 4)
        moved = fixed + (places - fixed + rotation * (used - fixed)) % max(1, count - fixed)
        return jnp.zeros((count,), jnp.int32).at[sequence[jnp.where(places < fixed, places, moved)]].set(jnp.asarray(sizes, jnp.int32))

    sizes = jnp.where(number % 4 == 0, named(heavy_load, number // 4), named(ordinary, number - number // 4 - 1))
    mixed = jax.random.permutation(jax.random.fold_in(own, 3), count)
    donor, receiver = mixed[0:count // 2 * 2:2], mixed[1:count // 2 * 2:2]
    room = jnp.minimum(sizes[donor] - 1, most - sizes[receiver]) // 2
    room = jnp.where((donor == sequence[0]) | (receiver == sequence[0]) | (sizes[receiver] == 0), 0, jnp.maximum(room, 0))
    moved = jax.random.randint(jax.random.fold_in(own, 4), (count // 2,), 0, 1 << 20) % (room + 1)
    sizes = sizes.at[donor].add(-moved).at[receiver].add(moved)
    items = jnp.searchsorted(jnp.cumsum(sizes), jnp.arange(rows * top), side="right").astype(jnp.int32)
    grid = items.reshape(top, rows).T
    grid = grid[jax.random.permutation(jax.random.fold_in(own, 1), rows)]
    rotation = jax.random.randint(jax.random.fold_in(own, 2), (rows, 1), 0, top)
    return jnp.take_along_axis(grid, (jnp.arange(top)[None, :] + rotation) % top, axis=1)


def load_shares(amount, total, most, lean, full):
    weights = [(1 << 20) // math.isqrt(standing ** lean) + 1 for standing in range(1, amount + 1)]
    largest = most if full else min(most, max(-(-total // amount), total * weights[0] // sum(weights)))
    least = 1 if total - largest >= amount - 1 else 0
    holding, surplus = [largest] + [least] * (amount - 1), total - largest - least * (amount - 1)
    while surplus > 0:
        movable = [i for i in range(1, amount) if holding[i] < largest] or [i for i in range(1, amount) if holding[i] < most]
        mass, budget = sum([weights[i] for i in movable]), surplus
        for i in movable:
            more = min(most - holding[i], max(1, budget * weights[i] // mass), surplus)
            holding[i] = holding[i] + more
            surplus = surplus - more
    return np.array(holding)


def bell_draw(key, dims, scale, reach, shards=(), kind=jnp.bfloat16):
    values = jax.random.normal(key, dims, jnp.float32) * scale
    if len(shards) > 0:
        values = shard_levels(key, dims, shards, -0.22, 0.18) * values
    return jnp.clip(values, min=-reach, max=reach).astype(kind)


def setup_inputs(seed: int = 0, part: int = 0) -> dict:
    key_list = jax.random.split(jax.random.key(seed), 17)
    own_keys = jax.random.split(jax.random.fold_in(key_list[16], part), 17)
    camera_features = bell_draw(own_keys[0], (BLOCKS, PTS, C0), 1.0, 6.0, ((0, 8),))
    cell_index = plant(jax.random.randint(own_keys[1], (BLOCKS, PTS), 0, TILE), jax.random.fold_in(own_keys[1], 1), 0, TILE - 1).astype(jnp.int32)
    owner_device_keys = jax.random.split(jax.random.fold_in(own_keys[2], 1), BLOCKS // BLK_DEV)
    owner_device_turns = jax.random.permutation(jax.random.fold_in(own_keys[2], 3), BLOCKS // BLK_DEV)
    owner_device = jax.vmap(lambda own, number: routed_block(jax.random.fold_in(own_keys[2], 2), own, number, BLK_DEV, N_SLAB, 1, CAP, 2))(owner_device_keys, owner_device_turns).reshape((BLOCKS, 1))
    owner_tile = plant(jax.random.randint(own_keys[3], (BLOCKS,), 0, TILES_DEV), jax.random.fold_in(own_keys[3], 1), 0, TILES_DEV - 1).astype(jnp.int32)
    base_map = bell_draw(own_keys[4], (ROWS, W, C0), 1.0, 6.0, ((0, 8),))
    targets = jnp.clip(1.0 * jax.random.uniform(own_keys[5], (ROWS, W, K), jnp.float32) ** shard_levels(own_keys[5], (ROWS, W, K), ((0, 8),), -0.2, 0.2), 0.0, 1.0).astype(jnp.bfloat16)
    fine_conv = bell_draw(key_list[6], (9 * C0, C0), (9 * C0) ** -0.5, 0.1875)
    fine_down = bell_draw(key_list[7], (4 * C0, C1), (4 * C0) ** -0.5, 0.25)
    middle_conv = bell_draw(key_list[8], (9 * C1, C1), (9 * C1) ** -0.5, 0.125)
    middle_down = bell_draw(key_list[9], (4 * C1, C2), (4 * C1) ** -0.5, 0.1875)
    coarse_conv = bell_draw(key_list[10], (9 * C2, C2), (9 * C2) ** -0.5, 0.09375)
    coarse_up = bell_draw(key_list[11], (C2, 4 * C1), C2 ** -0.5, 0.25)
    middle_merge = bell_draw(key_list[12], (9 * C1, C1), (9 * C1) ** -0.5, 0.125)
    middle_up = bell_draw(key_list[13], (C1, 4 * C0), C1 ** -0.5, 0.375)
    fine_merge = bell_draw(key_list[14], (9 * C0, C0), (9 * C0) ** -0.5, 0.1875)
    head_weight = bell_draw(key_list[15], (C0, K), C0 ** -0.5, 0.5)
    return {"camera_features": camera_features, "cell_index": cell_index, "owner_device": owner_device, "owner_tile": owner_tile, "base_map": base_map, "targets": targets, "fine_conv": fine_conv, "fine_down": fine_down, "middle_conv": middle_conv, "middle_down": middle_down, "coarse_conv": coarse_conv, "coarse_up": coarse_up, "middle_merge": middle_merge, "middle_up": middle_up, "fine_merge": fine_merge, "head_weight": head_weight}


loss_weight = 0.0625


def window_taps(padded):
    height = padded.shape[0] - 2
    across = padded.shape[1]
    framed = jnp.pad(padded, ((0, 0), (1, 1), (0, 0)))
    pieces = [framed[1 + row_step:1 + row_step + height, 1 + column_step:1 + column_step + across]
              for row_step in (-1, 0, 1) for column_step in (-1, 0, 1)]
    return jnp.concatenate(pieces, axis=-1).reshape(height * across, -1)


def flipped(weight):
    inward = weight.shape[0] // 9
    return weight.reshape(9, inward, -1)[::-1].transpose(0, 2, 1).reshape(-1, inward)


def fold_pairs(field):
    height, across, channels = field.shape
    return field.reshape(height // 2, 2, across // 2, 2, channels).transpose(0, 2, 1, 3, 4).reshape(
        (height // 2) * (across // 2), 4 * channels)


def unfold_pairs(matrix, height, across):
    channels = matrix.shape[1] // 4
    return matrix.reshape(height, across, 2, 2, channels).transpose(0, 2, 1, 3, 4).reshape(
        2 * height, 2 * across, channels)


def silu_slope(signal):
    logistic = jax.nn.sigmoid(signal)
    return logistic * (1.0 + signal * (1.0 - logistic))


def outer(former, latter):
    return lax.dot_general(former, latter, (((0,), (0,)), ((), ())), preferred_element_type=jnp.float32)


def backward(former, latter):
    return lax.dot_general(former, latter, (((1,), (1,)), ((), ())), preferred_element_type=jnp.float32)


def conv_whole(field, weight):
    padded = jnp.pad(field, ((1, 1), (0, 0), (0, 0)))
    taps = window_taps(padded)
    result = jnp.dot(taps, weight, preferred_element_type=jnp.float32)
    return result.reshape(field.shape[0], field.shape[1], -1), taps


def reference(camera_features, cell_index, owner_device, owner_tile, base_map, targets, fine_conv, fine_down,
              middle_conv, middle_down, coarse_conv, coarse_up, middle_merge, middle_up, fine_merge, head_weight):
    single = jnp.float32
    bfloat = jnp.bfloat16
    cell_onehot = (cell_index[:, :, None] == jnp.arange(TILE, dtype=jnp.int32)[None, None, :]).astype(single)
    deposits = jnp.einsum("bpt,bpc->btc", cell_onehot, camera_features.astype(single)).astype(bfloat)
    tile_number = (owner_device[:, 0] * TILES_DEV + owner_tile).astype(jnp.int32)
    canvas = jax.ops.segment_sum(deposits.astype(single).reshape(BLOCKS, -1), tile_number,
                                 num_segments=N_SLAB * TILES_DEV)
    level_zero = (base_map.astype(single) + canvas.reshape(ROWS, W, C0)).astype(bfloat)

    half_height, half_across = ROWS // 2, W // 2
    quarter_height, quarter_across = ROWS // 4, W // 4

    pre_fine, taps_fine = conv_whole(level_zero, fine_conv)
    hidden_fine = jax.nn.silu(pre_fine).astype(bfloat)
    quarter_fine = fold_pairs(hidden_fine)
    level_one = jnp.dot(quarter_fine, fine_down, preferred_element_type=single).astype(bfloat).reshape(
        half_height, half_across, C1)
    pre_middle, taps_middle = conv_whole(level_one, middle_conv)
    hidden_middle = jax.nn.silu(pre_middle).astype(bfloat)
    quarter_middle = fold_pairs(hidden_middle)
    level_two = jnp.dot(quarter_middle, middle_down, preferred_element_type=single).astype(bfloat).reshape(
        quarter_height, quarter_across, C2)
    pre_coarse, taps_coarse = conv_whole(level_two, coarse_conv)
    hidden_coarse = jax.nn.silu(pre_coarse).astype(bfloat)
    lifted = jnp.dot(hidden_coarse.reshape(-1, C2), coarse_up, preferred_element_type=single)
    joined_middle = (unfold_pairs(lifted, quarter_height, quarter_across)
                     + hidden_middle.astype(single)).astype(bfloat)
    pre_merge, taps_merge = conv_whole(joined_middle, middle_merge)
    out_middle = jax.nn.silu(pre_merge).astype(bfloat)
    raised = jnp.dot(out_middle.reshape(-1, C1), middle_up, preferred_element_type=single)
    joined_fine = (unfold_pairs(raised, half_height, half_across) + hidden_fine.astype(single)).astype(bfloat)
    pre_top, taps_top = conv_whole(joined_fine, fine_merge)
    out_fine = jax.nn.silu(pre_top).astype(bfloat)
    logits = jnp.dot(out_fine.reshape(-1, C0), head_weight, preferred_element_type=single)
    labels = targets.reshape(-1, K).astype(single)
    penalty = jax.nn.softplus(logits) - labels * logits
    row_loss = jnp.sum(penalty.reshape(ROWS, -1), axis=1) / (W * K)

    slope_logits = ((jax.nn.sigmoid(logits) - labels) * loss_weight).astype(bfloat)
    head_grad = outer(out_fine.reshape(-1, C0), slope_logits)
    back_top = (backward(slope_logits, head_weight) * silu_slope(pre_top.reshape(-1, C0))).astype(bfloat)
    fine_merge_grad = outer(taps_top, back_top)
    gradient_fine, _ = conv_whole(back_top.reshape(ROWS, W, C0), flipped(fine_merge))
    joined_fine_grad = gradient_fine.astype(bfloat)
    folded_fine_grad = fold_pairs(joined_fine_grad)
    middle_up_grad = outer(out_middle.reshape(-1, C1), folded_fine_grad)
    back_merge = (backward(folded_fine_grad, middle_up) * silu_slope(pre_merge.reshape(-1, C1))).astype(bfloat)
    middle_merge_grad = outer(taps_merge, back_merge)
    gradient_middle, _ = conv_whole(back_merge.reshape(half_height, half_across, C1), flipped(middle_merge))
    joined_middle_grad = gradient_middle.astype(bfloat)
    folded_middle_grad = fold_pairs(joined_middle_grad)
    coarse_up_grad = outer(hidden_coarse.reshape(-1, C2), folded_middle_grad)
    back_coarse = (backward(folded_middle_grad, coarse_up) * silu_slope(pre_coarse.reshape(-1, C2))).astype(bfloat)
    coarse_conv_grad = outer(taps_coarse, back_coarse)
    gradient_coarse, _ = conv_whole(back_coarse.reshape(quarter_height, quarter_across, C2), flipped(coarse_conv))
    level_two_grad = gradient_coarse.astype(bfloat)
    middle_down_grad = outer(quarter_middle, level_two_grad.reshape(-1, C2))
    spread = unfold_pairs(backward(level_two_grad.reshape(-1, C2), middle_down), quarter_height, quarter_across)
    back_middle = ((joined_middle_grad.astype(single) + spread) * silu_slope(pre_middle)).astype(bfloat)
    middle_conv_grad = outer(taps_middle, back_middle.reshape(-1, C1))
    gradient_one, _ = conv_whole(back_middle, flipped(middle_conv))
    level_one_grad = gradient_one.astype(bfloat)
    fine_down_grad = outer(quarter_fine, level_one_grad.reshape(-1, C1))
    spread_fine = unfold_pairs(backward(level_one_grad.reshape(-1, C1), fine_down), half_height, half_across)
    back_fine = ((joined_fine_grad.astype(single) + spread_fine) * silu_slope(pre_fine)).astype(bfloat)
    fine_conv_grad = outer(taps_fine, back_fine.reshape(-1, C0))
    gradient_zero, _ = conv_whole(back_fine, flipped(fine_conv))
    level_zero_grad = gradient_zero.astype(bfloat)

    tiles_grad = level_zero_grad.reshape(N_SLAB * TILES_DEV, TILE, C0)
    picked = tiles_grad[tile_number]
    camera_grad = jnp.einsum("bpt,btc->bpc", cell_onehot, picked.astype(single)).astype(bfloat)
    return (camera_grad, row_loss, fine_conv_grad, fine_down_grad, middle_conv_grad, middle_down_grad,
            coarse_conv_grad, coarse_up_grad, middle_merge_grad, middle_up_grad, fine_merge_grad, head_grad)
```

```python
import jax
import jax.numpy as jnp
from jax import lax
from jax.sharding import PartitionSpec as P

BLK_DEV = 64
C1 = 256
C2 = 512
K = 128
PTS = 128
TILE = 128
CAP = 8


loss_weight = 0.0625


def extended(block, sides, width):
    for axis, dim in sides:
        count = lax.axis_size(axis)
        forward = [(i, i + 1) for i in range(count - 1)]
        backward = [(target, source) for source, target in forward]
        low = lax.ppermute(
            lax.slice_in_dim(block, block.shape[dim] - width, None, axis=dim), axis, forward
        )
        high = lax.ppermute(lax.slice_in_dim(block, 0, width, axis=dim), axis, backward)
        block = jnp.concatenate([low, block, high], axis=dim)
    return block


def window_taps(padded):
    height = padded.shape[0] - 2
    across = padded.shape[1]
    framed = jnp.pad(padded, ((0, 0), (1, 1), (0, 0)))
    pieces = [
        framed[1 + row_step : 1 + row_step + height, 1 + column_step : 1 + column_step + across]
        for row_step in (-1, 0, 1)
        for column_step in (-1, 0, 1)
    ]
    return jnp.concatenate(pieces, axis=-1).reshape(height * across, -1)


def flipped(weight):
    inward = weight.shape[0] // 9
    return weight.reshape(9, inward, -1)[::-1].transpose(0, 2, 1).reshape(-1, inward)


def fold_pairs(field):
    height, across, channels = field.shape
    return (
        field.reshape(height // 2, 2, across // 2, 2, channels)
        .transpose(0, 2, 1, 3, 4)
        .reshape(height // 2 * (across // 2), 4 * channels)
    )


def unfold_pairs(matrix, height, across):
    channels = matrix.shape[1] // 4
    return (
        matrix.reshape(height, across, 2, 2, channels)
        .transpose(0, 2, 1, 3, 4)
        .reshape(2 * height, 2 * across, channels)
    )


def silu_slope(signal):
    logistic = jax.nn.sigmoid(signal)
    return logistic * (1.0 + signal * (1.0 - logistic))


def outer(former, latter):
    return lax.dot_general(
        former, latter, (((0,), (0,)), ((), ())), preferred_element_type=jnp.float32
    )


def backward(former, latter):
    return lax.dot_general(
        former, latter, (((1,), (1,)), ((), ())), preferred_element_type=jnp.float32
    )


def ring_reduce_scatter(grads, count, device):
    single, bfloat = (jnp.float32, jnp.bfloat16)
    pieces, spans = ([], [])
    for grad in grads:
        rows = grad.shape[0] // count
        part = grad.astype(bfloat).reshape(count, rows, grad.shape[1])
        for column in range(0, grad.shape[1], 128):
            pieces.append(part[:, :, column : column + 128])
        spans.append((rows, grad.shape[1] // 128))
    packed = jnp.concatenate(pieces, axis=1)
    total = packed.shape[1]
    cut = (total // 2 + 15) // 16 * 16
    ring = list(range(0, count, 2)) + list(range(count - 1, 0, -2))
    place = jnp.array([ring.index(i) for i in range(count)], jnp.int32)[device]
    order = jnp.array(ring, jnp.int32)
    ahead = [(ring[i], ring[(i + 1) % count]) for i in range(count)]
    behind = [(target, source) for source, target in ahead]

    def chunk(position, low, high):
        row = order[jnp.mod(position, count)]
        return lax.dynamic_index_in_dim(packed, row, 0, keepdims=False)[low:high]

    up = chunk(place - 1, 0, cut)
    down = chunk(place + 1, cut, total)
    for step in range(1, count):
        up = lax.ppermute(up, "slab", ahead)
        down = lax.ppermute(down, "slab", behind)
        up = up.astype(single) + chunk(place - 1 - step, 0, cut).astype(single)
        down = down.astype(single) + chunk(place + 1 + step, cut, total).astype(single)
        if step < count - 1:
            up, down = (up.astype(bfloat), down.astype(bfloat))
    joined = jnp.concatenate([up, down], axis=0)
    results, start = ([], 0)
    for rows, columns in spans:
        parts = [joined[start + i * rows : start + (i + 1) * rows] for i in range(columns)]
        results.append(jnp.concatenate(parts, axis=1))
        start += rows * columns
    return results


def rim_conv(field, weight):
    height, across = (field.shape[0], field.shape[1])
    padded = extended(field, (("slab", 0),), 1)
    middle_taps = window_taps(field)
    middle_out = jnp.dot(middle_taps, weight, preferred_element_type=jnp.float32)
    top_taps = window_taps(padded[0:3])
    taps_list = [top_taps]
    outs_list = [jnp.dot(top_taps, weight, preferred_element_type=jnp.float32)]
    taps_list.append(middle_taps)
    outs_list.append(middle_out)
    bottom_taps = window_taps(padded[height - 1 : height + 2])
    taps_list.append(bottom_taps)
    outs_list.append(jnp.dot(bottom_taps, weight, preferred_element_type=jnp.float32))
    taps = jnp.concatenate(taps_list, axis=0)
    result = jnp.concatenate(outs_list, axis=0)
    return (result.reshape(height, across, -1), taps)


def body(
    camera_features,
    cell_index,
    owner_device,
    owner_tile,
    base_map,
    targets,
    fine_conv,
    fine_down,
    middle_conv,
    middle_down,
    coarse_conv,
    coarse_up,
    middle_merge,
    middle_up,
    fine_merge,
    head_weight,
):
    single = jnp.float32
    bfloat = jnp.bfloat16
    device = lax.axis_index("slab")
    devices = lax.axis_size("slab")
    height, across, channels = base_map.shape
    slot_count = devices * CAP
    tile_count = height * across // TILE
    owners = owner_device[:, 0]
    everyone = owners.shape[0]
    choose = (owners[:, None] == jnp.arange(devices, dtype=jnp.int32)[None, :]).astype(jnp.int32)
    grouped = choose.reshape(devices, BLK_DEV, devices)
    earlier = (jnp.cumsum(grouped, axis=1) - grouped).reshape(everyone, devices)
    ranking = jnp.sum(earlier * choose, axis=1)
    sources = jnp.arange(everyone, dtype=jnp.int32) // BLK_DEV
    slot_number = owners * CAP + ranking
    local_slot = lax.dynamic_slice_in_dim(slot_number, device * BLK_DEV, BLK_DEV)
    slot_range = jnp.arange(slot_count, dtype=jnp.int32)
    send_map = (local_slot[None, :] == slot_range[:, None]).astype(bfloat)
    arrival = sources * CAP + ranking
    receive_map = ((arrival[None, :] == slot_range[:, None]) & (owners[None, :] == device)).astype(
        jnp.int32
    )
    tile_onehot = (owner_tile[:, None] == jnp.arange(tile_count, dtype=jnp.int32)[None, :]).astype(
        jnp.int32
    )
    placement = jnp.einsum("bt,sb->ts", tile_onehot, receive_map).astype(bfloat)
    cell_range = jnp.arange(TILE, dtype=jnp.int32)
    payload = camera_features.reshape(BLK_DEV, -1)
    outgoing = (
        jnp.dot(send_map, payload, preferred_element_type=single)
        .astype(bfloat)
        .reshape(devices, CAP, -1)
    )
    incoming = lax.all_to_all(outgoing, "slab", split_axis=0, concat_axis=0, tiled=True).reshape(
        slot_count, -1
    )
    slot_cells = jnp.dot(receive_map, cell_index)
    slot_onehot = (slot_cells[:, :, None] == cell_range[None, None, :]).astype(bfloat)
    deposits = (
        jnp.einsum(
            "spt,spc->stc",
            slot_onehot,
            incoming.reshape(slot_count, PTS, channels),
            preferred_element_type=single,
        )
        .astype(bfloat)
        .reshape(slot_count, -1)
    )
    canvas = jnp.dot(placement, deposits, preferred_element_type=single).reshape(
        height, across, channels
    )
    level_zero = (base_map.astype(single) + canvas).astype(bfloat)
    half_height, half_across = (height // 2, across // 2)
    quarter_height, quarter_across = (height // 4, across // 4)
    pre_fine, taps_fine = rim_conv(level_zero, fine_conv)
    hidden_fine = jax.nn.silu(pre_fine).astype(bfloat)
    quarter_fine = fold_pairs(hidden_fine)
    level_one = (
        jnp.dot(quarter_fine, fine_down, preferred_element_type=single)
        .astype(bfloat)
        .reshape(half_height, half_across, C1)
    )
    pre_middle, taps_middle = rim_conv(level_one, middle_conv)
    hidden_middle = jax.nn.silu(pre_middle).astype(bfloat)
    quarter_middle = fold_pairs(hidden_middle)
    level_two = (
        jnp.dot(quarter_middle, middle_down, preferred_element_type=single)
        .astype(bfloat)
        .reshape(quarter_height, quarter_across, C2)
    )
    pre_coarse, taps_coarse = rim_conv(level_two, coarse_conv)
    hidden_coarse = jax.nn.silu(pre_coarse).astype(bfloat)
    lifted = jnp.dot(hidden_coarse.reshape(-1, C2), coarse_up, preferred_element_type=single)
    joined_middle = (
        unfold_pairs(lifted, quarter_height, quarter_across) + hidden_middle.astype(single)
    ).astype(bfloat)
    pre_merge, taps_merge = rim_conv(joined_middle, middle_merge)
    out_middle = jax.nn.silu(pre_merge).astype(bfloat)
    raised = jnp.dot(out_middle.reshape(-1, C1), middle_up, preferred_element_type=single)
    joined_fine = (
        unfold_pairs(raised, half_height, half_across) + hidden_fine.astype(single)
    ).astype(bfloat)
    pre_top, taps_top = rim_conv(joined_fine, fine_merge)
    out_fine = jax.nn.silu(pre_top).astype(bfloat)
    logits = jnp.dot(out_fine.reshape(-1, channels), head_weight, preferred_element_type=single)
    labels = targets.reshape(-1, K).astype(single)
    penalty = jax.nn.softplus(logits) - labels * logits
    row_loss = jnp.sum(penalty.reshape(height, -1), axis=1) / (across * K)
    slope_logits = ((jax.nn.sigmoid(logits) - labels) * loss_weight).astype(bfloat)
    head_grad = outer(out_fine.reshape(-1, channels), slope_logits)
    back_top = (
        backward(slope_logits, head_weight) * silu_slope(pre_top.reshape(-1, channels))
    ).astype(bfloat)
    fine_merge_grad = outer(taps_top, back_top)
    gradient_fine, _ = rim_conv(back_top.reshape(height, across, channels), flipped(fine_merge))
    joined_fine_grad = gradient_fine.astype(bfloat)
    folded_fine_grad = fold_pairs(joined_fine_grad)
    middle_up_grad = outer(out_middle.reshape(-1, C1), folded_fine_grad)
    back_merge = (
        backward(folded_fine_grad, middle_up) * silu_slope(pre_merge.reshape(-1, C1))
    ).astype(bfloat)
    middle_merge_grad = outer(taps_merge, back_merge)
    gradient_middle, _ = rim_conv(
        back_merge.reshape(half_height, half_across, C1), flipped(middle_merge)
    )
    joined_middle_grad = gradient_middle.astype(bfloat)
    folded_middle_grad = fold_pairs(joined_middle_grad)
    coarse_up_grad = outer(hidden_coarse.reshape(-1, C2), folded_middle_grad)
    back_coarse = (
        backward(folded_middle_grad, coarse_up) * silu_slope(pre_coarse.reshape(-1, C2))
    ).astype(bfloat)
    gradient_coarse, _ = rim_conv(
        back_coarse.reshape(quarter_height, quarter_across, C2), flipped(coarse_conv)
    )
    level_two_grad = gradient_coarse.astype(bfloat)
    middle_down_grad = outer(quarter_middle, level_two_grad.reshape(-1, C2))
    spread = unfold_pairs(
        backward(level_two_grad.reshape(-1, C2), middle_down), quarter_height, quarter_across
    )
    back_middle = ((joined_middle_grad.astype(single) + spread) * silu_slope(pre_middle)).astype(
        bfloat
    )
    middle_conv_grad = outer(taps_middle, back_middle.reshape(-1, C1))
    gradient_one, _ = rim_conv(back_middle, flipped(middle_conv))
    level_one_grad = gradient_one.astype(bfloat)
    fine_down_grad = outer(quarter_fine, level_one_grad.reshape(-1, C1))
    spread_fine = unfold_pairs(
        backward(level_one_grad.reshape(-1, C1), fine_down), half_height, half_across
    )
    back_fine = ((joined_fine_grad.astype(single) + spread_fine) * silu_slope(pre_fine)).astype(
        bfloat
    )
    fine_conv_grad = outer(taps_fine, back_fine.reshape(-1, channels))
    gradient_zero, _ = rim_conv(back_fine, flipped(fine_conv))
    level_zero_grad = gradient_zero.astype(bfloat)
    tiles_grad = level_zero_grad.reshape(tile_count, -1)
    slot_grad = jnp.einsum(
        "ts,tl->sl", placement, tiles_grad, preferred_element_type=single
    ).astype(bfloat)
    returning = (
        jnp.einsum(
            "spt,stc->spc",
            slot_onehot,
            slot_grad.reshape(slot_count, TILE, channels),
            preferred_element_type=single,
        )
        .astype(bfloat)
        .reshape(slot_count, -1)
    )
    returned = lax.all_to_all(
        returning.reshape(devices, CAP, -1), "slab", split_axis=0, concat_axis=0, tiled=True
    ).reshape(slot_count, -1)
    own_blocks = jnp.einsum("sb,sl->bl", send_map, returned, preferred_element_type=single).astype(
        bfloat
    )
    camera_grad = own_blocks.reshape(BLK_DEV, PTS, channels)
    reduced = ring_reduce_scatter(
        (
            fine_conv_grad,
            fine_down_grad,
            middle_conv_grad,
            middle_down_grad,
            outer(taps_coarse, back_coarse),
            coarse_up_grad,
            middle_merge_grad,
            middle_up_grad,
            fine_merge_grad,
            head_grad,
        ),
        devices,
        device,
    )
    return (camera_grad, row_loss, *reduced)


def solution(mesh):
    return jax.shard_map(
        body,
        mesh=mesh,
        in_specs=(
            P(("scene", "slab"), None, None),
            P("scene", None),
            P("scene", None),
            P("scene"),
            P(("scene", "slab"), None, None),
            P(("scene", "slab"), None, None),
            P(),
            P(),
            P(),
            P(),
            P(),
            P(),
            P(),
            P(),
            P(),
            P(),
        ),
        out_specs=(
            P(("scene", "slab"), None, None),
            P(("scene", "slab")),
            P(("scene", "slab"), None),
            P(("scene", "slab"), None),
            P(("scene", "slab"), None),
            P(("scene", "slab"), None),
            P(("scene", "slab"), None),
            P(("scene", "slab"), None),
            P(("scene", "slab"), None),
            P(("scene", "slab"), None),
            P(("scene", "slab"), None),
            P(("scene", "slab"), None),
        ),
        check_vma=False,
    )
```

```python
import jax
import jax.numpy as jnp
from jax import lax
from jax.experimental import pallas as pl
from jax.experimental.pallas import tpu as pltpu
from jax.sharding import PartitionSpec as P

BLK_DEV = 64
TILE = 128
CAP = 8
LANES = 128
VMEM_BYTES = 60 * 1024 * 1024
INTERPRET = False

loss_weight = 0.0625

single = jnp.float32
bfloat = jnp.bfloat16


def call(kernel, name, outs, scratch, scalars, arrays):
    smem = pl.BlockSpec(memory_space=pltpu.SMEM)
    vmem = pl.BlockSpec(memory_space=pltpu.VMEM)
    return pl.pallas_call(
        kernel,
        name=name,
        out_shape=[jax.ShapeDtypeStruct(shape, dtype) for shape, dtype in outs],
        in_specs=[smem] * len(scalars) + [vmem] * len(arrays),
        out_specs=[vmem] * len(outs),
        scratch_shapes=[pltpu.VMEM(shape, dtype) for shape, dtype in scratch],
        compiler_params=pltpu.CompilerParams(vmem_limit_bytes=VMEM_BYTES),
        interpret=INTERPRET,
    )(*scalars, *arrays)


def loop(count, step):
    def wrapped(i, carry):
        step(i)
        return carry

    lax.fori_loop(0, count, wrapped, 0)


def block_of(total, most):
    return max(size for size in range(1, most + 1) if total % size == 0)


def zero_edges(flags, ref, rows):
    @pl.when(flags[0] == 0)
    def _():
        ref[0:rows] = jnp.zeros((rows,) + ref.shape[1:], ref.dtype)

    @pl.when(flags[1] == 0)
    def _():
        ref[ref.shape[0] - rows :] = jnp.zeros((rows,) + ref.shape[1:], ref.dtype)


def fill_sides(ref):
    rows, planes, cells, channels = ref.shape

    def step(r):
        place = lax.broadcasted_iota(jnp.int32, (cells, channels), 0)
        last = pltpu.roll(ref[r, planes - 2].astype(single), 1, 0)
        ref[r, 0] = jnp.where(place == 0, 0.0, last).astype(bfloat)
        first = pltpu.roll(ref[r, 1].astype(single), cells - 1, 0)
        ref[r, planes - 1] = jnp.where(place == cells - 1, 0.0, first).astype(bfloat)

    loop(rows, step)


def window(ref, row, count, first, planes):
    cells, channels = ref.shape[2:]
    return jnp.concatenate(
        [
            ref[pl.ds(row + down, count), first + k].reshape(count * cells, channels)
            for down in range(3)
            for k in range(planes)
        ],
        axis=1,
    )


def dot(a, b):
    return jnp.dot(a, b, preferred_element_type=single)


def dot_back(a, b):
    return lax.dot_general(a, b, (((1,), (1,)), ((), ())), preferred_element_type=single)


def dot_outer(a, b):
    return lax.dot_general(a, b, (((0,), (0,)), ((), ())), preferred_element_type=single)


def folded(ref, row, planes):
    half = ref.shape[1] // planes
    return [
        jnp.concatenate([ref[row + i, p * half + j] for i in range(2) for j in range(half)], axis=1)
        for p in range(planes)
    ]


def select_kernel(source, valid, blocks, out):
    def step(s):
        @pl.when(valid[s] > 0)
        def _():
            out[s] = blocks[source[s]]

        @pl.when(valid[s] == 0)
        def _():
            out[s] = jnp.zeros(out.shape[1:], out.dtype)

    loop(out.shape[0], step)


def splat_kernel(tiles, cells, incoming, base, level, top, bottom, canvas):
    slots = incoming.shape[0]
    rows, planes, across, channels = base.shape
    halves = across * planes // TILE
    part = TILE // planes

    def clear(t):
        canvas[t] = jnp.zeros(canvas.shape[1:], single)

    loop(canvas.shape[0], clear)

    def step(s):
        place = lax.broadcasted_iota(jnp.int32, (TILE, incoming.shape[1]), 0)
        hot = jnp.where(place == cells[s], 1.0, 0.0).astype(bfloat)
        deposit = dot(hot, incoming[s]).astype(bfloat).astype(single)
        t = tiles[s]
        canvas[t] = canvas[t] + deposit

    loop(slots, step)

    def settle(r):
        for h in range(halves):
            tile = canvas[r * halves + h]
            for m in range(planes):
                span = slice(h * part, (h + 1) * part)
                level[r, m, span] = (
                    base[r, m, span].astype(single) + tile[m * part : (m + 1) * part]
                ).astype(bfloat)

    loop(rows, settle)
    top[...] = level[0:3]
    bottom[...] = level[rows - 3 : rows]


def silu_pair(value):
    logistic = jax.nn.sigmoid(value)
    return (value * logistic).astype(bfloat), logistic * (1.0 + value * (1.0 - logistic))


def down_kernel(
    flags, level, above, below, fine_w, down_w, middle_w, middle_down_w,
    framed, hidden_fine, slope_fine, framed_one, hidden_middle, slope_middle, level_two,
    edge_top, edge_bottom,
):
    rows, _, cells, channels = level.shape
    framed[0:3, 1:5] = above[...]
    framed[3 : 3 + rows, 1:5] = level[...]
    framed[3 + rows :, 1:5] = below[...]
    fill_sides(framed)
    count = block_of(rows + 4, 4)

    def fine(i):
        row = i * count
        for pair in range(2):
            value = dot(window(framed, row, count, 2 * pair, 4), fine_w[...])
            hidden, slope = silu_pair(value)
            for k in range(2):
                lanes = slice(k * channels, (k + 1) * channels)
                shape = (count, cells, channels)
                hidden_fine[pl.ds(row, count), 2 * pair + k] = hidden[:, lanes].reshape(shape)
                slope_fine[pl.ds(row, count), 2 * pair + k] = (
                    slope[:, lanes].astype(bfloat).reshape(shape)
                )

    loop((rows + 4) // count, fine)
    zero_edges(flags, hidden_fine, 2)

    def lower(r):
        value = dot(jnp.concatenate(folded(hidden_fine, 2 * r, 2), axis=0), down_w[...])
        for p in range(2):
            framed_one[r, 1 + p] = value[p * cells : (p + 1) * cells].astype(bfloat)

    loop(rows // 2 + 2, lower)
    fill_sides(framed_one)
    half = rows // 2
    wide = block_of(half, 4)

    def middle(i):
        row = i * wide
        for p in range(2):
            value = dot(window(framed_one, row, wide, p, 3), middle_w[...])
            hidden, slope = silu_pair(value)
            shape = (wide, cells, value.shape[1])
            hidden_middle[pl.ds(row, wide), p] = hidden.reshape(shape)
            slope_middle[pl.ds(row, wide), p] = slope.astype(bfloat).reshape(shape)

    loop(half // wide, middle)

    def lowest(r):
        level_two[r] = dot(folded(hidden_middle, 2 * r, 1)[0], middle_down_w[...]).astype(bfloat)

    loop(rows // 4, lowest)
    quarter = rows // 4
    edge_top[0:2] = level_two[0:2]
    edge_bottom[0:2] = level_two[quarter - 2 : quarter]
    for i in range(2):
        edge_top[2 + i] = jnp.concatenate([hidden_middle[i, 0], hidden_middle[i, 1]], axis=1)
        edge_bottom[2 + i] = jnp.concatenate(
            [hidden_middle[half - 2 + i, 0], hidden_middle[half - 2 + i, 1]], axis=1
        )


def up_kernel(
    flags, level_two, above, below, hidden_middle, hidden_fine, targets,
    coarse_w, coarse_up_w, merge_w, up_w, top_w, head_w, top_flip,
    framed_two, hidden_coarse, slope_coarse, framed_joined, out_middle, framed_fine, framed_back,
    out_fine, slope_logits, loss, fine_grad, back_merge,
    merge_top, merge_bottom, fine_top, fine_bottom,
    slope_merge,
):
    quarter, cells, _ = level_two.shape
    half, rows = quarter * 2, quarter * 4
    channels = hidden_fine.shape[3]
    middle_channels = hidden_middle.shape[3]
    framed_two[0:2, 1] = above[0:2]
    framed_two[2 : 2 + quarter, 1] = level_two[...]
    framed_two[2 + quarter :, 1] = below[0:2]
    fill_sides(framed_two)
    count = block_of(quarter + 2, 3)

    def coarse(i):
        row = i * count
        value = dot(window(framed_two, row, count, 0, 3), coarse_w[...])
        hidden, slope = silu_pair(value)
        shape = (count, cells, value.shape[1])
        hidden_coarse[pl.ds(row, count)] = hidden.reshape(shape)
        slope_coarse[pl.ds(row, count)] = slope.astype(bfloat).reshape(shape)

    loop((quarter + 2) // count, coarse)
    zero_edges(flags, hidden_coarse, 1)

    for p in range(2):
        lanes = slice(p * middle_channels, (p + 1) * middle_channels)
        framed_joined[0:2, 1 + p] = above[2:4, :, lanes]
        framed_joined[2 : 2 + half, 1 + p] = hidden_middle[:, p]
        framed_joined[2 + half :, 1 + p] = below[2:4, :, lanes]

    def lift(r):
        value = dot(hidden_coarse[r], coarse_up_w[...])
        for i in range(2):
            for j in range(2):
                lanes = slice((2 * i + j) * middle_channels, (2 * i + j + 1) * middle_channels)
                skip = framed_joined[2 * r + i, 1 + j].astype(single)
                framed_joined[2 * r + i, 1 + j] = (value[:, lanes] + skip).astype(bfloat)

    loop(quarter + 2, lift)
    fill_sides(framed_joined)
    wide = block_of(half + 2, 5)

    def merge(i):
        row = i * wide
        for p in range(2):
            value = dot(window(framed_joined, row, wide, p, 3), merge_w[...])
            hidden, slope = silu_pair(value)
            shape = (wide, cells, middle_channels)
            out_middle[pl.ds(row, wide), p] = hidden.reshape(shape)
            slope_merge[pl.ds(row, wide), p] = slope.astype(bfloat).reshape(shape)

    loop((half + 2) // wide, merge)
    zero_edges(flags, out_middle, 1)

    def rise(r):
        value = dot(out_middle[r].reshape(2 * cells, middle_channels), up_w[...])
        for p in range(2):
            for i in range(2):
                for j in range(2):
                    lanes = slice((2 * i + j) * channels, (2 * i + j + 1) * channels)
                    skip = hidden_fine[2 * r + i, 2 * p + j].astype(single)
                    framed_fine[2 * r + i, 1 + 2 * p + j] = (
                        value[p * cells : (p + 1) * cells, lanes] + skip
                    ).astype(bfloat)

    loop(half + 2, rise)
    fill_sides(framed_fine)
    tall = block_of(rows + 2, 3)

    def top(i):
        row = i * tall
        for pair in range(2):
            value = dot(window(framed_fine, row, tall, 2 * pair, 4), top_w[...])
            hidden, slope = silu_pair(value)
            logits = dot(hidden, head_w[...])
            labels = jnp.concatenate(
                [
                    targets[pl.ds(row, tall), 2 * pair + k].reshape(tall * cells, channels)
                    for k in range(2)
                ],
                axis=1,
            ).astype(single)
            decay = jnp.exp(-jnp.abs(logits))
            penalty = jnp.maximum(logits, 0.0) + jnp.log1p(decay) - labels * logits
            share = 1.0 / (1.0 + decay)
            logistic = jnp.where(logits >= 0.0, share, decay * share)
            slopes = ((logistic - labels) * loss_weight).astype(bfloat)
            back = (dot_back(slopes, head_w[...]) * slope).astype(bfloat)
            sums = jnp.sum(penalty.reshape(tall, cells // 8, 8, 2 * channels), axis=1)
            sums = sums[:, :, :channels] + sums[:, :, channels:]
            if pair == 0:
                loss[pl.ds(row, tall)] = sums
            else:
                loss[pl.ds(row, tall)] = loss[pl.ds(row, tall)] + sums
            for k in range(2):
                lanes = slice(k * channels, (k + 1) * channels)
                shape = (tall, cells, channels)
                plane = 2 * pair + k
                out_fine[pl.ds(row, tall), plane] = hidden[:, lanes].reshape(shape)
                slope_logits[pl.ds(row, tall), plane] = slopes[:, lanes].reshape(shape)
                framed_back[pl.ds(row, tall), 1 + plane] = back[:, lanes].reshape(shape)

    loop((rows + 2) // tall, top)
    zero_edges(flags, framed_back, 1)
    fill_sides(framed_back)
    block = block_of(rows, 4)

    def spread(i):
        row = i * block
        for pair in range(2):
            value = dot(window(framed_back, row, block, 2 * pair, 4), top_flip[...]).astype(bfloat)
            for k in range(2):
                lanes = slice(k * channels, (k + 1) * channels)
                fine_grad[pl.ds(row, block), 2 * pair + k] = value[:, lanes].reshape(
                    block, cells, channels
                )

    loop(rows // block, spread)

    def lower(r):
        value = dot_back(jnp.concatenate(folded(fine_grad, 2 * r, 2), axis=0), up_w[...])
        for p in range(2):
            slope = slope_merge[r + 1, p].astype(single)
            back_merge[r, p] = (value[p * cells : (p + 1) * cells] * slope).astype(bfloat)

    loop(half, lower)
    merge_top[...] = back_merge[0:3]
    merge_bottom[...] = back_merge[half - 3 : half]
    fine_top[...] = fine_grad[0:1]
    fine_bottom[...] = fine_grad[rows - 1 : rows]


def turn_kernel(
    flags, back_merge, above, below, slope_coarse, slope_middle,
    merge_flip, coarse_up_w, coarse_flip, middle_down_w,
    joined_grad, framed_coarse, level_grad, back_middle, edge_top, edge_bottom,
    framed_merge,
):
    half, _, cells, channels = back_merge.shape
    quarter = half // 2
    framed_merge[0:3, 1:3] = above[...]
    framed_merge[3 : 3 + half, 1:3] = back_merge[...]
    framed_merge[3 + half :, 1:3] = below[...]
    fill_sides(framed_merge)
    wide = block_of(half + 4, 4)

    def merge(i):
        row = i * wide
        for p in range(2):
            value = dot(window(framed_merge, row, wide, p, 3), merge_flip[...])
            joined_grad[pl.ds(row, wide), p] = value.astype(bfloat).reshape(wide, cells, channels)

    loop((half + 4) // wide, merge)

    def lower(r):
        value = dot_back(folded(joined_grad, 2 * r, 1)[0], coarse_up_w[...])
        framed_coarse[r, 1] = (value * slope_coarse[r].astype(single)).astype(bfloat)

    loop(quarter + 2, lower)
    zero_edges(flags, framed_coarse, 1)
    fill_sides(framed_coarse)
    count = block_of(quarter, 4)

    def coarse(i):
        row = i * count
        value = dot(window(framed_coarse, row, count, 0, 3), coarse_flip[...])
        level_grad[pl.ds(row, count)] = value.astype(bfloat).reshape(count, cells, value.shape[1])

    loop(quarter // count, coarse)

    def lift(r):
        value = dot_back(level_grad[r], middle_down_w[...])
        for i in range(2):
            for j in range(2):
                lanes = slice((2 * i + j) * channels, (2 * i + j + 1) * channels)
                total = value[:, lanes] + joined_grad[2 * r + i + 2, j].astype(single)
                slope = slope_middle[2 * r + i, j].astype(single)
                back_middle[2 * r + i, j] = (total * slope).astype(bfloat)

    loop(quarter, lift)
    edge_top[...] = back_middle[0:2]
    edge_bottom[...] = back_middle[half - 2 : half]


def last_kernel(
    flags, tiles, back_middle, above, below, fine_grad, fine_above, fine_below, slope_fine, onehot,
    middle_flip, down_w, fine_flip,
    level_grad, framed_back, returning,
    framed_middle, tile_grad,
):
    half, _, cells, middle_channels = back_middle.shape
    rows, planes, _, channels = fine_grad.shape
    halves = cells * planes // TILE
    part = TILE // planes
    framed_middle[0:2, 1:3] = above[...]
    framed_middle[2 : 2 + half, 1:3] = back_middle[...]
    framed_middle[2 + half :, 1:3] = below[...]
    fill_sides(framed_middle)
    wide = block_of(half + 2, 5)

    def middle(i):
        row = i * wide
        for p in range(2):
            value = dot(window(framed_middle, row, wide, p, 3), middle_flip[...])
            level_grad[pl.ds(row, wide), p] = value.astype(bfloat).reshape(
                wide, cells, middle_channels
            )

    loop((half + 2) // wide, middle)
    blank = jnp.zeros((1, planes, cells, channels), bfloat)
    framed_back[0:1, 1:5] = blank
    framed_back[1:2, 1:5] = fine_above[...]
    framed_back[2 : 2 + rows, 1:5] = fine_grad[...]
    framed_back[2 + rows : 3 + rows, 1:5] = fine_below[...]
    framed_back[3 + rows :, 1:5] = blank

    def rise(r):
        value = dot_back(level_grad[r].reshape(2 * cells, middle_channels), down_w[...])
        for p in range(2):
            for i in range(2):
                for j in range(2):
                    lanes = slice((2 * i + j) * channels, (2 * i + j + 1) * channels)
                    plane = 2 * p + j
                    total = value[p * cells : (p + 1) * cells, lanes] + framed_back[
                        2 * r + i, 1 + plane
                    ].astype(single)
                    slope = slope_fine[2 * r + i, plane].astype(single)
                    framed_back[2 * r + i, 1 + plane] = (total * slope).astype(bfloat)

    loop(half + 2, rise)
    zero_edges(flags, framed_back, 2)
    fill_sides(framed_back)
    block = block_of(rows, 4)

    def fine(i):
        row = i * block
        for pair in range(2):
            value = dot(window(framed_back, row + 1, block, 2 * pair, 4), fine_flip[...])
            value = value.astype(bfloat)
            for r in range(block):
                for h in range(halves):
                    for k in range(2):
                        start = r * cells + h * part
                        plane = 2 * pair + k
                        tile_grad[(row + r) * halves + h, plane * part : (plane + 1) * part] = value[
                            start : start + part, k * channels : (k + 1) * channels
                        ]

    loop(rows // block, fine)

    def pick(s):
        returning[s] = dot(onehot[s], tile_grad[tiles[s]]).astype(bfloat)

    loop(returning.shape[0], pick)


def fine_taps_grad(acc, out, channels):
    for down in range(3):
        for side in range(3):
            total = sum(
                acc[
                    k * channels : (k + 1) * channels,
                    (4 * down + side + k) * channels : (4 * down + side + k + 1) * channels,
                ]
                for k in range(2)
            )
            tap = 3 * down + side
            out[tap * channels : (tap + 1) * channels] = total.T.astype(bfloat)


def fine_taps_sum(acc, back, back_row, framed, row, rows):
    cells, channels = framed.shape[2:]
    acc[...] = jnp.zeros(acc.shape, single)
    block = block_of(rows, 8)

    def step(i):
        for pair in range(2):
            pieces = [
                back[pl.ds(back_row + i * block, block), 1 + 2 * pair + k].reshape(
                    block * cells, channels
                )
                for k in range(2)
            ]
            taps = window(framed, row + i * block, block, 2 * pair, 4)
            acc[...] = acc[...] + dot_outer(jnp.concatenate(pieces, axis=1), taps)

    loop(rows // block, step)


def middle_taps_sum(acc, back, framed, row, rows):
    cells, channels = framed.shape[2:]
    acc[...] = jnp.zeros(acc.shape, single)
    block = block_of(rows, 4)

    def step(i):
        for p in range(2):
            piece = back[pl.ds(i * block, block), p].reshape(block * cells, channels)
            taps = window(framed, row + i * block, block, p, 3)
            acc[...] = acc[...] + dot_outer(piece, taps)

    loop(rows // block, step)


def middle_taps_grad(acc, out, channels):
    for tap in range(9):
        span = slice(tap * channels, (tap + 1) * channels)
        out[span] = acc[:, span].T.astype(bfloat)


def top_grads_kernel(
    framed_fine, framed_back, out_fine, slope_logits, out_middle, fine_grad,
    fine_merge_grad, head_grad, middle_up_grad,
    acc, head_acc, up_acc,
):
    rows, planes, cells, channels = fine_grad.shape
    half = rows // 2
    fine_taps_sum(acc, framed_back, 1, framed_fine, 1, rows)
    fine_taps_grad(acc, fine_merge_grad, channels)
    head_acc[...] = jnp.zeros(head_acc.shape, single)
    block = block_of(rows, 4)

    def head(i):
        span = pl.ds(1 + i * block, block)
        flat = (block * planes * cells, channels)
        head_acc[...] = head_acc[...] + dot_outer(
            out_fine[span].reshape(flat), slope_logits[span].reshape(flat)
        )

    loop(rows // block, head)
    head_grad[...] = head_acc[...].astype(bfloat)
    up_acc[...] = jnp.zeros(up_acc.shape, single)

    def rise(r):
        former = out_middle[r + 1].reshape(2 * cells, out_middle.shape[3])
        latter = jnp.concatenate(folded(fine_grad, 2 * r, 2), axis=0)
        up_acc[...] = up_acc[...] + dot_outer(former, latter)

    loop(half, rise)
    middle_up_grad[...] = up_acc[...].astype(bfloat)


def coarse_grads_kernel(
    framed_joined, back_merge, framed_two, framed_coarse, hidden_coarse, joined_grad,
    hidden_middle, level_grad,
    middle_merge_grad, coarse_conv_grad, coarse_up_grad, middle_down_grad,
    acc,
):
    quarter, cells, channels = level_grad.shape
    half = 2 * quarter
    middle_taps_sum(acc, back_merge, framed_joined, 1, half)
    middle_taps_grad(acc, middle_merge_grad, framed_joined.shape[3])
    flat = (quarter * cells, channels)
    back = framed_coarse[1 : 1 + quarter, 1].reshape(flat)
    for down in range(3):
        for side in range(3):
            tap = 3 * down + side
            piece = framed_two[1 + down : 1 + down + quarter, side].reshape(flat)
            coarse_conv_grad[tap * channels : (tap + 1) * channels] = dot_outer(
                piece, back
            ).astype(bfloat)
    latter = jnp.concatenate([folded(joined_grad, 2 * r + 2, 1)[0] for r in range(quarter)], axis=0)
    coarse_up_grad[...] = dot_outer(
        hidden_coarse[1 : 1 + quarter].reshape(flat), latter
    ).astype(bfloat)
    former = jnp.concatenate([folded(hidden_middle, 2 * r, 1)[0] for r in range(quarter)], axis=0)
    middle_down_grad[...] = dot_outer(former, level_grad[...].reshape(flat)).astype(bfloat)


def base_grads_kernel(
    framed, framed_back, framed_one, back_middle, hidden_fine, level_grad,
    fine_conv_grad, middle_conv_grad, fine_down_grad,
    acc, middle_acc, down_acc,
):
    half, _, cells, middle_channels = back_middle.shape
    rows = 2 * half
    fine_taps_sum(acc, framed_back, 2, framed, 2, rows)
    fine_taps_grad(acc, fine_conv_grad, framed.shape[3])
    middle_taps_sum(middle_acc, back_middle, framed_one, 0, half)
    middle_taps_grad(middle_acc, middle_conv_grad, middle_channels)
    down_acc[...] = jnp.zeros(down_acc.shape, single)

    def lower(r):
        former = jnp.concatenate(folded(hidden_fine, 2 * r + 2, 2), axis=0)
        latter = level_grad[r + 1].reshape(2 * cells, middle_channels)
        down_acc[...] = down_acc[...] + dot_outer(former, latter)

    loop(half, lower)
    fine_down_grad[...] = down_acc[...].astype(bfloat)


def ring_reduce_scatter(grads, count, device):
    pieces, spans = ([], [])
    for grad in grads:
        rows = grad.shape[0] // count
        part = grad.astype(bfloat).reshape(count, rows, grad.shape[1])
        for column in range(0, grad.shape[1], LANES):
            pieces.append(part[:, :, column : column + LANES])
        spans.append((rows, grad.shape[1] // LANES))
    packed = jnp.concatenate(pieces, axis=1)
    total = packed.shape[1]
    cut = (total // 2 + 15) // 16 * 16
    ring = list(range(0, count, 2)) + list(range(count - 1, 0, -2))
    place = jnp.array([ring.index(i) for i in range(count)], jnp.int32)[device]
    order = jnp.array(ring, jnp.int32)
    ahead = [(ring[i], ring[(i + 1) % count]) for i in range(count)]
    behind = [(target, source) for source, target in ahead]

    def chunk(position, low, high):
        row = order[jnp.mod(position, count)]
        return lax.dynamic_index_in_dim(packed, row, 0, keepdims=False)[low:high]

    up = chunk(place - 1, 0, cut)
    down = chunk(place + 1, cut, total)
    for step in range(1, count):
        up = lax.ppermute(up, "slab", ahead)
        down = lax.ppermute(down, "slab", behind)
        up = up.astype(single) + chunk(place - 1 - step, 0, cut).astype(single)
        down = down.astype(single) + chunk(place + 1 + step, cut, total).astype(single)
        if step < count - 1:
            up, down = (up.astype(bfloat), down.astype(bfloat))
    joined = jnp.concatenate([up, down], axis=0)
    results, start = ([], 0)
    for rows, columns in spans:
        parts = [joined[start + i * rows : start + (i + 1) * rows] for i in range(columns)]
        results.append(jnp.concatenate(parts, axis=1))
        start += rows * columns
    return results


def flipped(weight):
    inward = weight.shape[0] // 9
    return weight.reshape(9, inward, -1)[::-1].transpose(0, 2, 1).reshape(-1, inward)


def paired(weight):
    taps = weight.reshape(3, 3, weight.shape[0] // 9, weight.shape[1])
    columns = [jnp.pad(taps, ((0, 0), (k, 1 - k), (0, 0), (0, 0))) for k in range(2)]
    return jnp.concatenate(columns, axis=3).reshape(12 * taps.shape[2], 2 * taps.shape[3])


def phased(field):
    height, across, channels = field.shape
    return field.reshape(height, across // 4, 4, channels).transpose(0, 2, 1, 3)


def body(
    camera_features,
    cell_index,
    owner_device,
    owner_tile,
    base_map,
    targets,
    fine_conv,
    fine_down,
    middle_conv,
    middle_down,
    coarse_conv,
    coarse_up,
    middle_merge,
    middle_up,
    fine_merge,
    head_weight,
):
    device = lax.axis_index("slab")
    devices = lax.axis_size("slab")
    height, across, channels = base_map.shape
    cells = across // 4
    half, quarter = (height // 2, height // 4)
    c1, c2 = (fine_down.shape[1], middle_down.shape[1])
    points = camera_features.shape[1]
    slots = devices * CAP
    tile_count = height * across // TILE
    forward = [(i, i + 1) for i in range(devices - 1)]
    reverse = [(target, source) for source, target in forward]

    def exchange(top, bottom):
        return lax.ppermute(bottom, "slab", forward), lax.ppermute(top, "slab", reverse)

    flags = jnp.stack([device > 0, device < devices - 1]).astype(jnp.int32)
    owners = owner_device[:, 0]
    everyone = owners.shape[0]
    choose = (owners[:, None] == jnp.arange(devices, dtype=jnp.int32)[None, :]).astype(jnp.int32)
    grouped = choose.reshape(devices, BLK_DEV, devices)
    earlier = (jnp.cumsum(grouped, axis=1) - grouped).reshape(everyone, devices)
    ranking = jnp.sum(earlier * choose, axis=1)
    sources = jnp.arange(everyone, dtype=jnp.int32) // BLK_DEV
    local_slot = lax.dynamic_slice_in_dim(owners * CAP + ranking, device * BLK_DEV, BLK_DEV)
    slot_range = jnp.arange(slots, dtype=jnp.int32)
    sends = (local_slot[None, :] == slot_range[:, None]).astype(jnp.int32)
    send_block = jnp.sum(sends * jnp.arange(BLK_DEV, dtype=jnp.int32)[None, :], axis=1)
    send_valid = jnp.sum(sends, axis=1)
    (outgoing,) = call(
        select_kernel, "pack_blocks", [((slots, points, channels), bfloat)], [],
        [send_block, send_valid], [camera_features],
    )
    incoming = lax.all_to_all(outgoing, "slab", split_axis=0, concat_axis=0, tiled=True)

    receive = (
        ((sources * CAP + ranking)[None, :] == slot_range[:, None]) & (owners[None, :] == device)
    ).astype(jnp.int32)
    tiles = jnp.sum(receive * owner_tile[None, :], axis=1)
    slot_cells = jnp.dot(
        receive.astype(bfloat), cell_index.astype(bfloat), preferred_element_type=single
    ).astype(jnp.int32)
    slot_cells = slot_cells % 4 * (TILE // 4) + slot_cells // 4
    onehot = (
        slot_cells[:, :, None] == jnp.arange(TILE, dtype=jnp.int32)[None, None, :]
    ).astype(bfloat)
    target_above, target_below = exchange(targets[:1], targets[height - 1 :])
    labels = phased(jnp.concatenate([target_above, targets, target_below], axis=0))
    base = phased(base_map)
    fine_pair, top_pair = (paired(fine_conv), paired(fine_merge))
    fine_flip, top_flip = (paired(flipped(fine_conv)), paired(flipped(fine_merge)))
    middle_flip, merge_flip = (flipped(middle_conv), flipped(middle_merge))
    coarse_flip = flipped(coarse_conv)
    blank = jnp.zeros_like(head_weight)
    head_pair = jnp.concatenate(
        [
            jnp.concatenate([head_weight, blank], axis=1),
            jnp.concatenate([blank, head_weight], axis=1),
        ],
        axis=0,
    )

    fine_row = (4, cells, channels)
    middle_row = (2, cells, c1)
    coarse_row = (cells, c2)
    level_zero, top, bottom = call(
        splat_kernel, "splat",
        [((height,) + fine_row, bfloat), ((3,) + fine_row, bfloat), ((3,) + fine_row, bfloat)],
        [((tile_count, TILE, channels), single)],
        [tiles], [slot_cells[:, None, :], incoming, base],
    )
    above, below = exchange(top, bottom)
    (
        framed_zero, hidden_fine, slope_fine, framed_one, hidden_middle, slope_middle, level_two,
        top, bottom,
    ) = call(
        down_kernel, "down",
        [
            ((height + 6, 6, cells, channels), bfloat),
            ((height + 4,) + fine_row, bfloat),
            ((height + 4,) + fine_row, bfloat),
            ((half + 2, 4, cells, c1), bfloat),
            ((half,) + middle_row, bfloat),
            ((half,) + middle_row, bfloat),
            ((quarter,) + coarse_row, bfloat),
            ((4,) + coarse_row, bfloat),
            ((4,) + coarse_row, bfloat),
        ],
        [], [flags], [level_zero, above, below, fine_pair, fine_down, middle_conv, middle_down],
    )
    above, below = exchange(top, bottom)
    (
        framed_two, hidden_coarse, slope_coarse, framed_joined, out_middle, framed_fine,
        framed_top, out_fine, slope_logits, loss, fine_grad, back_merge,
        merge_top, merge_bottom, fine_top, fine_bottom,
    ) = call(
        up_kernel, "up",
        [
            ((quarter + 4, 3) + coarse_row, bfloat),
            ((quarter + 2,) + coarse_row, bfloat),
            ((quarter + 2,) + coarse_row, bfloat),
            ((half + 4, 4, cells, c1), bfloat),
            ((half + 2,) + middle_row, bfloat),
            ((height + 4, 6, cells, channels), bfloat),
            ((height + 2, 6, cells, channels), bfloat),
            ((height + 2,) + fine_row, bfloat),
            ((height + 2,) + fine_row, bfloat),
            ((height + 2, 8, channels), single),
            ((height,) + fine_row, bfloat),
            ((half,) + middle_row, bfloat),
            ((3,) + middle_row, bfloat),
            ((3,) + middle_row, bfloat),
            ((1,) + fine_row, bfloat),
            ((1,) + fine_row, bfloat),
        ],
        [((half + 2,) + middle_row, bfloat)],
        [flags],
        [
            level_two, above, below, hidden_middle, hidden_fine, labels,
            coarse_conv, coarse_up, middle_merge, middle_up, top_pair, head_pair, top_flip,
        ],
    )
    row_loss = jnp.sum(loss[1 : 1 + height], axis=(1, 2)) / (across * channels)
    above, below = exchange(merge_top, merge_bottom)
    fine_above, fine_below = exchange(fine_top, fine_bottom)
    fine_merge_grad, head_grad, middle_up_grad = call(
        top_grads_kernel, "top_grads",
        [
            (fine_merge.shape, bfloat),
            (head_weight.shape, bfloat),
            (middle_up.shape, bfloat),
        ],
        [
            ((2 * channels, 12 * channels), single),
            (head_weight.shape, single),
            (middle_up.shape, single),
        ],
        [], [framed_fine, framed_top, out_fine, slope_logits, out_middle, fine_grad],
    )
    joined_grad, framed_coarse, level_two_grad, back_middle, top, bottom = call(
        turn_kernel, "turn",
        [
            ((half + 4,) + middle_row, bfloat),
            ((quarter + 2, 3) + coarse_row, bfloat),
            ((quarter,) + coarse_row, bfloat),
            ((half,) + middle_row, bfloat),
            ((2,) + middle_row, bfloat),
            ((2,) + middle_row, bfloat),
        ],
        [((half + 6, 4, cells, c1), bfloat)],
        [flags],
        [
            back_merge, above, below, slope_coarse, slope_middle,
            merge_flip, coarse_up, coarse_flip, middle_down,
        ],
    )
    above, below = exchange(top, bottom)
    middle_merge_grad, coarse_conv_grad, coarse_up_grad, middle_down_grad = call(
        coarse_grads_kernel, "coarse_grads",
        [
            (middle_merge.shape, bfloat),
            (coarse_conv.shape, bfloat),
            (coarse_up.shape, bfloat),
            (middle_down.shape, bfloat),
        ],
        [((c1, 9 * c1), single)],
        [],
        [
            framed_joined, back_merge, framed_two, framed_coarse, hidden_coarse, joined_grad,
            hidden_middle, level_two_grad,
        ],
    )
    level_one_grad, framed_base, returning = call(
        last_kernel, "last",
        [
            ((half + 2,) + middle_row, bfloat),
            ((height + 4, 6, cells, channels), bfloat),
            ((slots, points, channels), bfloat),
        ],
        [((half + 4, 4, cells, c1), bfloat), ((tile_count, TILE, channels), bfloat)],
        [flags, tiles],
        [
            back_middle, above, below, fine_grad, fine_above, fine_below, slope_fine, onehot,
            middle_flip, fine_down, fine_flip,
        ],
    )
    returned = lax.all_to_all(returning, "slab", split_axis=0, concat_axis=0, tiled=True)
    fine_conv_grad, middle_conv_grad, fine_down_grad = call(
        base_grads_kernel, "base_grads",
        [(fine_conv.shape, bfloat), (middle_conv.shape, bfloat), (fine_down.shape, bfloat)],
        [
            ((2 * channels, 12 * channels), single),
            ((c1, 9 * c1), single),
            (fine_down.shape, single),
        ],
        [], [framed_zero, framed_base, framed_one, back_middle, hidden_fine, level_one_grad],
    )
    (camera_grad,) = call(
        select_kernel, "unpack_blocks", [(camera_features.shape, bfloat)], [],
        [local_slot, jnp.ones_like(local_slot)], [returned],
    )
    reduced = ring_reduce_scatter(
        (
            fine_conv_grad,
            fine_down_grad,
            middle_conv_grad,
            middle_down_grad,
            coarse_conv_grad,
            coarse_up_grad,
            middle_merge_grad,
            middle_up_grad,
            fine_merge_grad,
            head_grad,
        ),
        devices,
        device,
    )
    return (camera_grad, row_loss, *reduced)


def solution(mesh):
    split = P(("scene", "slab"))
    return jax.shard_map(
        body,
        mesh=mesh,
        in_specs=(
            split, P("scene"), P("scene"), P("scene"), split, split,
            P(), P(), P(), P(), P(), P(), P(), P(), P(), P(),
        ),
        out_specs=(split,) * 12,
        check_vma=False,
    )
```
